32 devices in a mesh: dp: 8 (over z, y), mp: 4 (over x, core).
Axes of the slice: x: 2, y: 2, z: 4, core: 2. Of those that a mesh axis runs over, the one named last changes fastest.
Arguments:
- hidden: bfloat16 [8192, 5120], P('dp'), may hold values from -6 to 6
- exit_depth: int32 [8192], P('dp'), may hold values from 0 to 3, as said below
- seq_ids: int32 [8192], P('dp'), may hold values from 0 to 3, as said below
- dest: int32 [8192], P('dp'), may hold values from 0 to 7, as said below
- norm_gain: bfloat16 [5120], replicated, may hold values from 0.5 to 1.5
- w_query: bfloat16 [5120, 3072], P(None, 'mp'), may hold values from -4 to 4
- w_key: bfloat16 [5120, 3072], P(None, 'mp'), may hold values from -4 to 4
- w_value: bfloat16 [5120, 3072], P(None, 'mp'), may hold values from -0.078125 to 0.078125
- w_out: bfloat16 [3072, 5120], P('mp'), may hold values from -0.4375 to 0.4375
Outputs:
- next_rows: bfloat16 [6144, 5120], P('dp', 'mp')
The draws below stay inside these ranges and needn't reach their ends.
Inputs may be any that keep to these rules, and one draw needn't show every extreme that they name: exit_depth is 3 for at most 768 tokens of one sequence, and for exactly that many in some sequence. seq_ids never fall along a sequence. `dest`: within one sequence, at most 96 tokens with exit depth 3 name the same destination, and some sequence has exactly 96 that do.
All inputs are finite; a program needn't handle non-finite values.
Results may differ from the reference program's by a relative error of at most 0.014.
Values may be sent and summed in bfloat16 or wider, within the bound.
A program may use at most 128 MiB of HBM per device.

```python
import math
import jax
import jax.numpy as jnp
from jax import lax

D = 5120
HD = 128
HEADS = 24
TOK_DEV = 1024
HW = 3072
TOKENS = 8192
SLOTS = 768
CAP = 96
N_DP = 8
N_MP = 4


def routing_plan(key):
    base = jax.random.fold_in(key, 4242)
    key_level, key_forced, key_rows, key_buckets, key_spare, key_depth = jax.random.split(base, 6)
    level = jax.random.randint(key_level, (N_DP,), 1, 13)
    forced = jax.random.randint(key_forced, (), 0, N_DP)
    level = jnp.where(jnp.arange(N_DP) == forced, 12, level)
    counts = level * (TOK_DEV // 16)

    def row_order(sub_key):
        return jax.random.permutation(sub_key, TOK_DEV)

    def bucket_order(sub_key):
        return jax.random.permutation(sub_key, N_DP)
    ranks = jax.vmap(row_order)(jax.random.split(key_rows, N_DP))
    buckets = jax.vmap(bucket_order)(jax.random.split(key_buckets, N_DP))
    active = ranks < counts[:, None]
    bucket = jnp.minimum(ranks // CAP, N_DP - 1)
    live_dest = jnp.take_along_axis(buckets, bucket, axis=1)
    spare = jax.random.randint(key_spare, (N_DP, TOK_DEV), 0, N_DP)
    target = jnp.where(active, live_dest, spare)
    depth = jnp.where(active, 3, jax.random.randint(key_depth, (N_DP, TOK_DEV), 0, 3))
    return (depth.reshape(-1).astype(jnp.int32), target.reshape(-1).astype(jnp.int32))


def draw_exit_depth(key, part):
    return routing_plan(key)[0]


def draw_dest(key, part):
    return routing_plan(key)[1]


def draw_seq_ids(key, part):
    cut_key = jax.random.fold_in(key, 777)
    cuts = jax.random.randint(cut_key, (N_DP, 3), 1, TOK_DEV)
    places = jnp.arange(TOK_DEV)
    documents = jnp.sum((places[None, :, None] >= cuts[:, None, :]).astype(jnp.int32), axis=2)
    return documents.reshape(-1).astype(jnp.int32)


def projection_draw(key, salt):
    base_draw = jax.random.truncated_normal(jax.random.fold_in(key, salt), -6.0, 6.0, (D, HW), jnp.float32) / math.sqrt(D)
    return base_draw


def draw_w_query(key, part):
    return projection_draw(key, 31).astype(jnp.bfloat16)


def draw_w_key(key, part):
    return projection_draw(key, 32).astype(jnp.bfloat16)


def draw_hidden(key, part):
    noise_rows = jax.random.truncated_normal(jax.random.fold_in(key, 51), -6.0, 6.0, (N_DP, TOK_DEV, D), jnp.float32)
    return noise_rows.reshape(TOKENS, D).astype(jnp.bfloat16)


def block_levels(own_key, shape, pieces, smallest, high):
    factor_of, own = 1.0, jax.random.fold_in(own_key, 6)
    for dim, shards_of in pieces:
        steps = jnp.exp(jax.random.uniform(jax.random.fold_in(own, dim), (shards_of,), jnp.float32, smallest / len(pieces), high / len(pieces)))
        factor_of = factor_of * jnp.repeat(steps, shape[dim] // shards_of).reshape([-1 if axis == dim else 1 for axis in range(len(shape))])
    return factor_of


def noise(stream_key, shape, width, bound, pieces=(), held_as=jnp.bfloat16):
    values = width * jax.random.normal(stream_key, shape, jnp.float32)
    if pieces:
        values = values * block_levels(stream_key, shape, pieces, -0.22, 0.18)
    return jnp.clip(values, -bound, bound).astype(held_as)


def setup_inputs(seed: int = 0) -> dict:
    key_of = jax.random.split(jax.random.key(seed), 10)
    hidden = draw_hidden(jax.random.fold_in(key_of[9], 71), 0)
    exit_depth = draw_exit_depth(jax.random.fold_in(key_of[9], 71), 0)
    seq_ids = draw_seq_ids(jax.random.fold_in(key_of[9], 71), 0)
    dest = draw_dest(jax.random.fold_in(key_of[9], 71), 0)
    norm_gain = jnp.clip(1.0 + 0.1 * jax.random.normal(key_of[4], (D,), jnp.float32), 0.5, 1.5).astype(jnp.bfloat16)
    w_query = draw_w_query(jax.random.fold_in(key_of[9], 71), 0)
    w_key = draw_w_key(jax.random.fold_in(key_of[9], 71), 0)
    w_value = noise(key_of[7], (D, HW), D ** -0.5, 0.078125, ((1, 4),))
    w_out = noise(key_of[8], (HW, D), (HW // 16) ** -0.5, 0.4375, ((0, 4),))
    return {"hidden": hidden, "exit_depth": exit_depth, "seq_ids": seq_ids, "dest": dest, "norm_gain": norm_gain, "w_query": w_query, "w_key": w_key, "w_value": w_value, "w_out": w_out}


def rotate_pairs(values, places):
    half_width = values.shape[-1] // 2
    frequency = 10000.0 ** (-jnp.arange(half_width, dtype=jnp.float32) / half_width)
    angle = places[:, None] * frequency[None, :]
    cosine = jnp.cos(angle)[:, None, :]
    sine_term = jnp.sin(angle)[:, None, :]
    first = values[..., :half_width]
    second = values[..., half_width:]
    return jnp.concatenate([first * cosine - second * sine_term, second * cosine + first * sine_term], axis=-1)

def normalize(rows, norm_gain):
    widened = rows.astype(jnp.float32)
    mean_square = lax.optimization_barrier(jnp.mean(widened * widened, axis=-1, keepdims=True))
    return (widened * lax.rsqrt(mean_square + 1e-05) * norm_gain.astype(jnp.float32)).astype(jnp.bfloat16)

def reference(hidden, exit_depth, seq_ids, dest, norm_gain, w_query, w_key, w_value, w_out):
    scale_factor = 1.0 / math.sqrt(HD)
    places = jnp.arange(TOK_DEV, dtype=jnp.float32)
    group_width = HEADS * HD // N_MP
    out_groups = w_out.astype(jnp.float32).reshape(N_MP, group_width, D)

    def one_sequence(operands):
        rows, documents = operands
        normed = normalize(rows, norm_gain)

        def project(weight):
            return jnp.dot(normed, weight, preferred_element_type=jnp.float32).reshape(TOK_DEV, HEADS, HD)
        queries = rotate_pairs(project(w_query), places).astype(jnp.bfloat16)
        keys = rotate_pairs(project(w_key), places).astype(jnp.bfloat16)
        values = project(w_value).astype(jnp.bfloat16)
        scores = jnp.einsum('qhd,khd->hqk', queries.astype(jnp.float32), keys.astype(jnp.float32)) * scale_factor
        allowed = (documents[:, None] == documents[None, :]) & (places[None, :] <= places[:, None])
        scores = jnp.where(allowed[None], scores, -1e+30)
        highest = lax.optimization_barrier(jnp.max(scores, axis=-1, keepdims=True))
        raised = jnp.exp(scores - highest)
        probs = (raised / lax.optimization_barrier(jnp.sum(raised, axis=-1, keepdims=True))).astype(jnp.bfloat16)
        attended = jnp.einsum('hqk,khd->qhd', probs.astype(jnp.float32), values.astype(jnp.float32))
        attended = attended.astype(jnp.bfloat16).reshape(TOK_DEV, N_MP, group_width)
        partials = jnp.einsum('tgc,gcd->gtd', attended.astype(jnp.float32), out_groups)
        partials = lax.optimization_barrier(partials.astype(jnp.bfloat16)).astype(jnp.float32)
        return (rows.astype(jnp.float32) + lax.optimization_barrier(jnp.sum(partials, axis=0))).astype(jnp.bfloat16)
    updated = lax.map(one_sequence, (hidden.reshape(N_DP, TOK_DEV, D), seq_ids.reshape(N_DP, TOK_DEV)))
    active = (exit_depth == 3).reshape(N_DP, TOK_DEV)
    targets = dest.reshape(N_DP, TOK_DEV)
    chosen = ((targets[:, :, None] == jnp.arange(N_DP, dtype=jnp.int32)[None, None, :]) & active[:, :, None]).astype(jnp.int32)
    running = jnp.cumsum(chosen, axis=1)
    order_rank = lax.optimization_barrier(jnp.sum(running * chosen, axis=2)) - 1
    sources = jnp.arange(N_DP, dtype=jnp.int32)[:, None]
    slot_of = jnp.where(active, targets * SLOTS + sources * CAP + order_rank, N_DP * SLOTS).astype(jnp.int32)
    result = jnp.zeros((N_DP * SLOTS, D), jnp.bfloat16)
    return result.at[slot_of.reshape(-1)].set(updated.reshape(-1, D), mode='drop')
```

```python
import functools
import math

import jax
import jax.numpy as jnp
import numpy as np
from jax import lax
from jax.experimental import pallas as pl
from jax.experimental.pallas import tpu as pltpu
from jax.sharding import PartitionSpec as P

HD = 128
CHUNKS = 8
LAG = 1
LOAD_ROWS = 256
ANY = pl.ANY
VMEM = pltpu.VMEM


def rope_tables(tokens):
    half = HD // 2
    frequency = 10000.0 ** (-np.arange(half, dtype=np.float64) / half)
    angle = np.arange(tokens, dtype=np.float64)[:, None] * frequency[None, :]
    cosine, sine = np.cos(angle), np.sin(angle)
    return (
        np.concatenate([cosine, cosine], axis=1).astype(np.float32),
        np.concatenate([-sine, sine], axis=1).astype(np.float32),
    )


def layer_kernel(
    peers, groups, per_chunk, bn,
    depth_row, seq_row, dest_row, gain, cosine, sine, hidden, wq, wk, wv, w_out, out,
    normed, wbuf, qkv, obuf, residual, slot_row, pair_send, pair_recv, x_send, x_recv, acc, updated,
    hsem, wsem, osem, rsem, pair_ssem, pair_rsem, x_ssem, x_rsem, row_ssem, row_rsem, own_sem,
):
    chunks, ring, rows, feature_slice = pair_send.shape
    capacity = rows // per_chunk
    _, tokens, inner = qkv.shape
    blocks = inner // bn
    loads = tokens // LOAD_ROWS
    slots = wbuf.shape[0]
    d, m = lax.axis_index("dp"), lax.axis_index("mp")
    core, x = lax.rem(m, 2), m // 2
    partner = x * 2 + 1 - core
    query_scale = math.log2(math.e) / math.sqrt(HD)
    mesh_id = pl.DeviceIdType.MESH

    def x_to(r):
        return lax.rem(x + r, ring)

    def target(i):
        away = peers // 2 + ((i + 1) // 2) * (1 - 2 * lax.rem(i, 2))
        return lax.rem(d + away, peers)

    def fetch(index, do):
        for which, w in enumerate((wk, wv, wq)):

            @pl.when(index // blocks == which)
            def _():
                column = pl.multiple_of(lax.rem(index, blocks) * bn, bn)
                to = lax.rem(index, slots)
                do(pltpu.make_async_copy(w.at[:, pl.ds(column, bn)], wbuf.at[to], wsem.at[to]))

    def hidden_copy(r):
        part = pl.ds(r * LOAD_ROWS, LOAD_ROWS)
        return pltpu.make_async_copy(hidden.at[part], normed.at[part], hsem.at[r])

    def out_weight_copy(n):
        columns = pl.ds(n * feature_slice, feature_slice)
        return pltpu.make_async_copy(w_out.at[:, columns], obuf.at[n], osem.at[n])

    def residual_copy():
        columns = pl.ds(pl.multiple_of(m * feature_slice, HD), feature_slice)
        return pltpu.make_async_copy(hidden.at[:, columns], residual, rsem)

    def pair_copy(j, r):
        return pltpu.make_async_remote_copy(
            src_ref=pair_send.at[j, r], dst_ref=pair_recv.at[j, r],
            send_sem=pair_ssem.at[j, r], recv_sem=pair_rsem.at[j, r],
            device_id={"mp": partner}, device_id_type=mesh_id,
        )

    def x_copy(j, r):
        return pltpu.make_async_remote_copy(
            src_ref=x_send.at[j, r - 1], dst_ref=x_recv.at[j, r - 1],
            send_sem=x_ssem.at[j, r - 1], recv_sem=x_rsem.at[j, r - 1],
            device_id={"mp": x_to(r) * 2 + core}, device_id_type=mesh_id,
        )

    def own_rows():
        return out.at[pl.ds(pl.multiple_of(d * capacity, 16), capacity)]

    def row_copy(j, k):
        return pltpu.make_async_remote_copy(
            src_ref=updated.at[j, pl.ds(k * capacity, capacity)], dst_ref=own_rows(),
            send_sem=row_ssem.at[j, k], recv_sem=row_rsem.at[j, k],
            device_id={"dp": target(j * per_chunk + k)}, device_id_type=mesh_id,
        )

    def own_copy():
        return pltpu.make_async_copy(
            updated.at[chunks - 1, pl.ds(rows - capacity, capacity)], own_rows(), own_sem
        )

    hidden_copy(0).start()
    fetch(0, lambda c: c.start())
    for r in range(1, loads):
        hidden_copy(r).start()
    for index in range(1, slots):
        fetch(index, lambda c: c.start())

    barrier = pltpu.get_barrier_semaphore()
    for i in range(1, peers):
        pl.semaphore_signal(
            barrier, inc=1, device_id={"dp": lax.rem(d + i, peers)}, device_id_type=mesh_id
        )
    for r in range(1, ring):
        pl.semaphore_signal(
            barrier, inc=1, device_id={"mp": x_to(r) * 2 + core}, device_id_type=mesh_id
        )
    pl.semaphore_signal(barrier, inc=1, device_id={"mp": partner}, device_id_type=mesh_id)

    code = jnp.where(depth_row[...] == 3, dest_row[...], -1)
    hot_shape = (max(16, peers), tokens)
    lanes_of = lax.broadcasted_iota(jnp.int32, hot_shape, 1)
    hot = jnp.where(lax.broadcasted_iota(jnp.int32, hot_shape, 0) == code, 1.0, 0.0)
    count, shift = hot, 1
    while shift < tokens:
        count = count + jnp.where(lanes_of >= shift, pltpu.roll(count, shift, 1), 0.0)
        shift *= 2
    rank = jnp.sum(hot * count, axis=0, keepdims=True) - 1.0
    slot_row[...] = jnp.where(code >= 0, code * capacity + rank.astype(jnp.int32), -1)

    def store(y, part, which, column, rotate, scale=None):
        for h in range(bn // HD):
            lanes = slice(h * HD, (h + 1) * HD)
            z = y[:, lanes]
            if rotate:
                z = z * cosine[part, :] + pltpu.roll(z, HD // 2, 1) * sine[part, :]
            if scale is not None:
                z = z * scale
            qkv[which, part, pl.ds(pl.multiple_of(column + h * HD, HD), HD)] = z.astype(jnp.bfloat16)

    def first(r, carry):
        hidden_copy(r).wait()
        part = pl.ds(pl.multiple_of(r * LOAD_ROWS, LOAD_ROWS), LOAD_ROWS)
        v = normed[part, :].astype(jnp.float32)
        mean_square = jnp.mean(v * v, axis=-1, keepdims=True)
        y = v * lax.rsqrt(mean_square + 1e-05) * gain[...].astype(jnp.float32)[None, :]
        normed[part, :] = y.astype(jnp.bfloat16)

        @pl.when(r == 0)
        def _():
            fetch(0, lambda c: c.wait())

        y = jnp.dot(normed[part, :], wbuf[0], preferred_element_type=jnp.float32)
        store(y, part, 0, 0, True)
        return carry

    lax.fori_loop(0, loads, first, 0)

    def project(step, carry):
        @pl.when(step - 1 + slots < 3 * blocks)
        def _():
            fetch(step - 1 + slots, lambda c: c.start())

        @pl.when(step == 1)
        def _():
            residual_copy().start()
            for n in range(groups):
                out_weight_copy(n).start()

        fetch(step, lambda c: c.wait())
        slot = lax.rem(step, slots)
        which = step // blocks
        column = lax.rem(step, blocks) * bn
        everything = slice(0, tokens)
        for rotate in (True, False):

            @pl.when((which != 1) == rotate)
            def _():
                y = jnp.dot(normed[...], wbuf[slot], preferred_element_type=jnp.float32)
                if rotate:
                    store(y, everything, which, column, True, jnp.where(which == 2, query_scale, 1.0))
                else:
                    store(y, everything, 1, column, False)

        return carry

    lax.fori_loop(1, 3 * blocks, project, 0)

    for n in range(groups):
        out_weight_copy(n).wait()
    residual_copy().wait()
    pl.semaphore_wait(barrier, peers + ring - 1)

    def chosen(j):
        parts = []
        for k in range(per_chunk):
            row = lax.broadcasted_iota(jnp.int32, (capacity, tokens), 0)
            parts.append((row + target(j * per_chunk + k) * capacity) == slot_row[...])
        return jnp.concatenate(parts, axis=0) if per_chunk > 1 else parts[0]

    def attend(j):
        hit = chosen(j)
        places = lax.broadcasted_iota(jnp.int32, (rows, tokens), 1).astype(jnp.float32)
        weight = jnp.where(hit, 1.0, 0.0)
        pick = weight.astype(jnp.bfloat16)
        filled = jnp.sum(weight, axis=-1, keepdims=True)
        place = jnp.sum(jnp.where(hit, places, 0.0), axis=-1, keepdims=True)
        documents = seq_row[...].astype(jnp.float32)
        document = jnp.sum(jnp.where(hit, documents, 0.0), axis=-1, keepdims=True)
        allowed = (document == documents) & (places <= place)
        bias = jnp.where(allowed, 0.0, -1e30)
        queries = jnp.dot(pick, qkv[2], preferred_element_type=jnp.float32).astype(jnp.bfloat16)
        heads = []
        for h in range(inner // HD):
            lanes = slice(h * HD, (h + 1) * HD)
            scores = lax.dot_general(
                queries[:, lanes], qkv[0, :, lanes], (((1,), (1,)), ((), ())),
                preferred_element_type=jnp.float32,
            )
            scores = scores + bias
            raised = jnp.exp2(scores - jnp.max(scores, axis=-1, keepdims=True))
            total = jnp.sum(raised, axis=-1, keepdims=True)
            mixed = jnp.dot(
                raised.astype(jnp.bfloat16), qkv[1, :, lanes], preferred_element_type=jnp.float32
            )
            heads.append((mixed * (filled / total)).astype(jnp.bfloat16))
        return jnp.concatenate(heads, axis=1), pick

    def multiply(attended, n):
        return jnp.dot(attended, obuf[n], preferred_element_type=jnp.float32).astype(jnp.bfloat16)

    def step(s, carry):
        @pl.when(s < chunks)
        def _():
            attended, pick = attend(s)
            order = list(range(1, ring)) + [0]
            own = {}
            for r in order:
                pair_send[s, r] = multiply(attended, x_to(r) * 2 + 1 - core)
                pair_copy(s, r).start()
                own[r] = multiply(attended, x_to(r) * 2 + core).astype(jnp.float32)
                if r == 0:
                    kept = jnp.dot(pick, residual[...], preferred_element_type=jnp.float32)
                    acc[lax.rem(s, LAG + 1)] = kept + own[0]
                else:
                    pair_copy(s, r).wait_recv()
                    total = own[r] + pair_recv[s, r].astype(jnp.float32)
                    x_send[s, r - 1] = total.astype(jnp.bfloat16)
                    x_copy(s, r).start()

        @pl.when(s >= LAG)
        def _():
            j = s - LAG
            pair_copy(j, 0).wait_recv()
            total = acc[lax.rem(j, LAG + 1)] + pair_recv[j, 0].astype(jnp.float32)
            for r in range(1, ring):
                x_copy(j, r).wait_recv()
                total += x_recv[j, r - 1].astype(jnp.float32)
            updated[j] = total.astype(jnp.bfloat16)
            for k in range(per_chunk - 1):
                row_copy(j, k).start()

            @pl.when(j < chunks - 1)
            def _():
                row_copy(j, per_chunk - 1).start()

        return carry

    lax.fori_loop(0, chunks + LAG, step, 0)
    own_copy().start()

    def drain(j, carry):
        for r in range(ring):
            pair_copy(j, r).wait_send()
        for r in range(1, ring):
            x_copy(j, r).wait_send()
        for k in range(per_chunk - 1):
            row_copy(j, k).wait()

        @pl.when(j < chunks - 1)
        def _():
            row_copy(j, per_chunk - 1).wait()

        return carry

    lax.fori_loop(0, chunks, drain, 0)
    own_copy().wait()


def body(hidden, exit_depth, seq_ids, dest, norm_gain, w_query, w_key, w_value, w_out):
    peers = lax.axis_size("dp")
    groups = lax.axis_size("mp")
    tokens, width = hidden.shape
    inner = w_query.shape[1]
    slots = 3 * tokens // 4
    feature_slice = w_out.shape[1] // groups
    chunks = min(CHUNKS, peers)
    rows = slots // chunks
    ring = groups // 2
    per_chunk = peers // chunks
    bn = 256 if inner % 256 == 0 else HD
    cosine, sine = rope_tables(tokens)
    dma = pltpu.SemaphoreType.DMA
    bf16 = jnp.bfloat16
    vmem = pl.BlockSpec(memory_space=VMEM)
    far = pl.BlockSpec(memory_space=ANY)
    line = lambda v: v.reshape(1, tokens)
    return pl.pallas_call(
        functools.partial(layer_kernel, peers, groups, per_chunk, bn),
        out_shape=jax.ShapeDtypeStruct((slots, feature_slice), bf16),
        in_specs=[vmem] * 6 + [far] * 5,
        out_specs=far,
        scratch_shapes=[
            VMEM((tokens, width), bf16),
            VMEM((3, width, bn), bf16),
            VMEM((3, tokens, inner), bf16),
            VMEM((groups, inner, feature_slice), bf16),
            VMEM((tokens, feature_slice), bf16),
            VMEM((1, tokens), jnp.int32),
            VMEM((chunks, ring, rows, feature_slice), bf16),
            VMEM((chunks, ring, rows, feature_slice), bf16),
            VMEM((chunks, ring - 1, rows, feature_slice), bf16),
            VMEM((chunks, ring - 1, rows, feature_slice), bf16),
            VMEM((LAG + 1, rows, feature_slice), jnp.float32),
            VMEM((chunks, rows, feature_slice), bf16),
            dma((tokens // LOAD_ROWS,)),
            dma((3,)),
            dma((groups,)),
            dma,
            dma((chunks, ring)),
            dma((chunks, ring)),
            dma((chunks, ring - 1)),
            dma((chunks, ring - 1)),
            dma((chunks, per_chunk)),
            dma((chunks, per_chunk)),
            dma,
        ],
        compiler_params=pltpu.CompilerParams(
            collective_id=0, has_side_effects=True, vmem_limit_bytes=60 * 2**20
        ),
        name="layer",
    )(
        line(exit_depth), line(seq_ids), line(dest), norm_gain, cosine, sine,
        hidden, w_query, w_key, w_value, w_out,
    )


def solution(mesh):
    return jax.shard_map(
        body,
        mesh=mesh,
        in_specs=(
            P("dp", None),
            P("dp"),
            P("dp"),
            P("dp"),
            P(),
            P(None, "mp"),
            P(None, "mp"),
            P(None, "mp"),
            P("mp", None),
        ),
        out_specs=P("dp", "mp"),
        check_vma=False,
    )
```

```python
import functools
import math

import jax
import jax.numpy as jnp
import numpy as np
from jax import lax
from jax.experimental import pallas as pl
from jax.experimental.pallas import tpu as pltpu
from jax.sharding import PartitionSpec as P

HD = 128
CHUNKS = 8
LAG = 1
LOAD_ROWS = 256
ANY = pl.ANY
VMEM = pltpu.VMEM


def rope_tables(tokens):
    half = HD // 2
    frequency = 10000.0 ** (-np.arange(half, dtype=np.float64) / half)
    angle = np.arange(tokens, dtype=np.float64)[:, None] * frequency[None, :]
    cosine, sine = np.cos(angle), np.sin(angle)
    return (
        np.concatenate([cosine, cosine], axis=1).astype(np.float32),
        np.concatenate([-sine, sine], axis=1).astype(np.float32),
    )


def layer_kernel(
    peers, groups, per_chunk, bn,
    depth_row, seq_row, dest_row, gain, rope, hidden, wq, wk, wv, w_out, out,
    normed, wbuf, qkv, obuf, residual, table, slot_row, pick, bias, mixed_rows,
    pair_send, pair_recv, x_send, x_recv, acc, updated,
    hsem, wsem, osem, rsem, tsem, pair_ssem, pair_rsem, x_ssem, x_rsem, row_ssem, row_rsem, own_sem,
):
    chunks, ring, halves, rows, half = pair_send.shape
    feature_slice = half * halves
    capacity = rows // per_chunk
    _, tokens, inner = qkv.shape
    blocks = inner // bn
    loads = tokens // LOAD_ROWS
    slots = wbuf.shape[0]
    d, m = lax.axis_index("dp"), lax.axis_index("mp")
    core, x = lax.rem(m, 2), m // 2
    partner = x * 2 + 1 - core
    query_scale = math.log2(math.e) / math.sqrt(HD)
    mesh_id = pl.DeviceIdType.MESH

    def x_to(r):
        return lax.rem(x + r, ring)

    def target(i):
        away = peers // 2 + ((i + 1) // 2) * (1 - 2 * lax.rem(i, 2))
        return lax.rem(d + away, peers)

    def fetch(index, do):
        for which, w in enumerate((wk, wv, wq)):

            @pl.when(index // blocks == which)
            def _():
                column = pl.multiple_of(lax.rem(index, blocks) * bn, bn)
                to = lax.rem(index, slots)
                do(pltpu.make_async_copy(w.at[:, pl.ds(column, bn)], wbuf.at[to], wsem.at[to]))

    def hidden_copy(r):
        part = pl.ds(r * LOAD_ROWS, LOAD_ROWS)
        return pltpu.make_async_copy(hidden.at[part], normed.at[part], hsem.at[r])

    def table_copy():
        return pltpu.make_async_copy(rope, table, tsem)

    def out_weight_copy(n, h):
        columns = pl.ds(n * feature_slice + h * half, half)
        return pltpu.make_async_copy(w_out.at[:, columns], obuf.at[n, h], osem.at[n, h])

    def residual_copy(h):
        columns = pl.ds(pl.multiple_of(m * feature_slice + h * half, HD), half)
        return pltpu.make_async_copy(hidden.at[:, columns], residual.at[h], rsem.at[h])

    def pair_copy(j, r, h):
        return pltpu.make_async_remote_copy(
            src_ref=pair_send.at[j, r, h], dst_ref=pair_recv.at[j, r, h],
            send_sem=pair_ssem.at[j, r, h], recv_sem=pair_rsem.at[j, r, h],
            device_id={"mp": partner}, device_id_type=mesh_id,
        )

    def x_copy(j, r, h):
        return pltpu.make_async_remote_copy(
            src_ref=x_send.at[j, r - 1, h], dst_ref=x_recv.at[j, r - 1, h],
            send_sem=x_ssem.at[j, r - 1, h], recv_sem=x_rsem.at[j, r - 1, h],
            device_id={"mp": x_to(r) * 2 + core}, device_id_type=mesh_id,
        )

    def own_rows(h):
        return out.at[pl.ds(pl.multiple_of(d * capacity, 16), capacity), pl.ds(h * half, half)]

    def row_copy(j, k, h):
        return pltpu.make_async_remote_copy(
            src_ref=updated.at[j, h, pl.ds(k * capacity, capacity)], dst_ref=own_rows(h),
            send_sem=row_ssem.at[j, k, h], recv_sem=row_rsem.at[j, k, h],
            device_id={"dp": target(j * per_chunk + k)}, device_id_type=mesh_id,
        )

    def own_copy(h):
        return pltpu.make_async_copy(
            updated.at[chunks - 1, h, pl.ds(rows - capacity, capacity)], own_rows(h), own_sem.at[h]
        )

    hidden_copy(0).start()
    fetch(0, lambda c: c.start())
    table_copy().start()
    hidden_copy(1).start()

    barrier = pltpu.get_barrier_semaphore()
    for i in range(1, peers):
        pl.semaphore_signal(
            barrier, inc=1, device_id={"dp": lax.rem(d + i, peers)}, device_id_type=mesh_id
        )
    for r in range(1, ring):
        pl.semaphore_signal(
            barrier, inc=1, device_id={"mp": x_to(r) * 2 + core}, device_id_type=mesh_id
        )
    pl.semaphore_signal(barrier, inc=1, device_id={"mp": partner}, device_id_type=mesh_id)

    code = jnp.where(depth_row[...] == 3, dest_row[...], -1)
    hot_shape = (max(16, peers), tokens)
    lanes_of = lax.broadcasted_iota(jnp.int32, hot_shape, 1)
    hot = jnp.where(lax.broadcasted_iota(jnp.int32, hot_shape, 0) == code, 1.0, 0.0)
    count, shift = hot, 1
    while shift < tokens:
        count = count + jnp.where(lanes_of >= shift, pltpu.roll(count, shift, 1), 0.0)
        shift *= 2
    rank = jnp.sum(hot * count, axis=0, keepdims=True) - 1.0
    slot_row[...] = jnp.where(code >= 0, code * capacity + rank.astype(jnp.int32), -1)

    def prepare(j):
        parts = []
        for k in range(per_chunk):
            row = lax.broadcasted_iota(jnp.int32, (capacity, tokens), 0)
            parts.append((row + target(j * per_chunk + k) * capacity) == slot_row[...])
        hit = jnp.concatenate(parts, axis=0) if per_chunk > 1 else parts[0]
        places = lax.broadcasted_iota(jnp.int32, (rows, tokens), 1).astype(jnp.float32)
        place = jnp.sum(jnp.where(hit, places, 0.0), axis=-1, keepdims=True)
        documents = seq_row[...].astype(jnp.float32)
        document = jnp.sum(jnp.where(hit, documents, 0.0), axis=-1, keepdims=True)
        allowed = (document == documents) & (places <= place)
        pick[...] = jnp.where(hit, 1.0, 0.0).astype(jnp.bfloat16)
        bias[...] = jnp.where(allowed, 0.0, -1e30)

    prepare(0)

    def store(y, part, which, column, rotate, scale=None):
        for h in range(bn // HD):
            lanes = slice(h * HD, (h + 1) * HD)
            z = y[:, lanes]
            if rotate:
                z = z * table[0, part, :] + pltpu.roll(z, HD // 2, 1) * table[1, part, :]
            if scale is not None:
                z = z * scale
            qkv[which, part, pl.ds(pl.multiple_of(column + h * HD, HD), HD)] = z.astype(jnp.bfloat16)

    def normalize(r):
        part = slice(r * LOAD_ROWS, (r + 1) * LOAD_ROWS)
        v = normed[part, :].astype(jnp.float32)
        mean_square = jnp.mean(v * v, axis=-1, keepdims=True)
        y = v * lax.rsqrt(mean_square + 1e-05) * gain[...].astype(jnp.float32)[None, :]
        normed[part, :] = y.astype(jnp.bfloat16)

    hidden_copy(0).wait()
    hidden_copy(2).start()
    normalize(0)
    fetch(0, lambda c: c.wait())
    table_copy().wait()
    for r in range(loads):
        part = slice(r * LOAD_ROWS, (r + 1) * LOAD_ROWS)
        if r + 1 < loads:
            hidden_copy(r + 1).wait()
        if r + 3 < loads:
            hidden_copy(r + 3).start()
        if 1 <= r < slots:
            fetch(r, lambda c: c.start())
        y = jnp.dot(normed[part, :], wbuf[0], preferred_element_type=jnp.float32)
        if r + 1 < loads:
            normalize(r + 1)
        store(y, part, 0, 0, True)

    def project(step, carry):
        @pl.when(step - 1 + slots < 3 * blocks)
        def _():
            fetch(step - 1 + slots, lambda c: c.start())

        @pl.when(step == 1)
        def _():
            for h in range(halves):
                residual_copy(h).start()
                for n in range(groups):
                    out_weight_copy(n, h).start()

        fetch(step, lambda c: c.wait())
        slot = lax.rem(step, slots)
        which = step // blocks
        column = lax.rem(step, blocks) * bn
        everything = slice(0, tokens)
        for rotate in (True, False):

            @pl.when((which != 1) == rotate)
            def _():
                y = jnp.dot(normed[...], wbuf[slot], preferred_element_type=jnp.float32)
                if rotate:
                    store(y, everything, which, column, True, jnp.where(which == 2, query_scale, 1.0))
                else:
                    store(y, everything, 1, column, False)

        return carry

    lax.fori_loop(1, 3 * blocks, project, 0)

    for h in range(halves):
        residual_copy(h).wait()
        for n in range(groups):
            out_weight_copy(n, h).wait()
    pl.semaphore_wait(barrier, peers + ring - 1)

    def attend():
        filled = jnp.sum(pick[...].astype(jnp.float32), axis=-1, keepdims=True)
        queries = jnp.dot(pick[...], qkv[2], preferred_element_type=jnp.float32).astype(jnp.bfloat16)
        for h in range(inner // HD):
            lanes = slice(h * HD, (h + 1) * HD)
            scores = lax.dot_general(
                queries[:, lanes], qkv[0, :, lanes], (((1,), (1,)), ((), ())),
                preferred_element_type=jnp.float32,
            )
            scores = scores + bias[...]
            raised = jnp.exp2(scores - jnp.max(scores, axis=-1, keepdims=True))
            total = jnp.sum(raised, axis=-1, keepdims=True)
            mixed = jnp.dot(
                raised.astype(jnp.bfloat16), qkv[1, :, lanes], preferred_element_type=jnp.float32
            )
            mixed_rows[:, lanes] = (mixed * (filled / total)).astype(jnp.bfloat16)

    def multiply(n, h):
        return jnp.dot(mixed_rows[...], obuf[n, h], preferred_element_type=jnp.float32).astype(
            jnp.bfloat16
        )

    def complete(j, h):
        pair_copy(j, 0, h).wait_recv()
        total = acc[lax.rem(j, LAG + 1), h] + pair_recv[j, 0, h].astype(jnp.float32)
        for r in range(1, ring):
            x_copy(j, r, h).wait_recv()
            total += x_recv[j, r - 1, h].astype(jnp.float32)
        updated[j, h] = total.astype(jnp.bfloat16)
        for k in range(per_chunk - 1):
            row_copy(j, k, h).start()

        @pl.when(j < chunks - 1)
        def _():
            row_copy(j, per_chunk - 1, h).start()

    def step(s, carry):
        @pl.when(s < chunks)
        def _():
            attend()
            for r in range(1, ring):
                for h in range(halves):
                    pair_send[s, r, h] = multiply(x_to(r) * 2 + 1 - core, h)
                    pair_copy(s, r, h).start()

        @pl.when(s >= LAG)
        def _():
            complete(s - LAG, 0)

        @pl.when(s < chunks)
        def _():
            for r in range(1, ring):
                for h in range(halves):
                    own = multiply(x_to(r) * 2 + core, h).astype(jnp.float32)
                    pair_copy(s, r, h).wait_recv()
                    total = own + pair_recv[s, r, h].astype(jnp.float32)
                    x_send[s, r - 1, h] = total.astype(jnp.bfloat16)
                    x_copy(s, r, h).start()
            for h in range(halves):
                pair_send[s, 0, h] = multiply(x * 2 + 1 - core, h)
                pair_copy(s, 0, h).start()
            for h in range(halves):
                kept = jnp.dot(pick[...], residual[h], preferred_element_type=jnp.float32)
                acc[lax.rem(s, LAG + 1), h] = kept + multiply(x * 2 + core, h).astype(jnp.float32)

        @pl.when(s >= LAG)
        def _():
            for h in range(1, halves):
                complete(s - LAG, h)

        @pl.when(s + 1 < chunks)
        def _():
            prepare(s + 1)

        return carry

    lax.fori_loop(0, chunks + LAG, step, 0)
    for h in range(halves):
        own_copy(h).start()

    def drain(j, carry):
        for h in range(halves):
            for r in range(ring):
                pair_copy(j, r, h).wait_send()
            for r in range(1, ring):
                x_copy(j, r, h).wait_send()
            for k in range(per_chunk - 1):
                row_copy(j, k, h).wait()

        @pl.when(j < chunks - 1)
        def _():
            for h in range(halves):
                row_copy(j, per_chunk - 1, h).wait()

        return carry

    lax.fori_loop(0, chunks, drain, 0)
    for h in range(halves):
        own_copy(h).wait()


def place_kernel(source, out, held, in_sem, out_sem):
    pieces, rows, _ = held.shape

    def load(i):
        return pltpu.make_async_copy(source.at[pl.ds(i * rows, rows)], held.at[i], in_sem.at[i])

    def save(i):
        return pltpu.make_async_copy(held.at[i], out.at[pl.ds(i * rows, rows)], out_sem.at[i])

    for i in range(pieces):
        load(i).start()
    for i in range(pieces):
        load(i).wait()
        save(i).start()
    for i in range(pieces):
        save(i).wait()


def body(hidden, exit_depth, seq_ids, dest, norm_gain, w_query, w_key, w_value, w_out):
    peers = lax.axis_size("dp")
    groups = lax.axis_size("mp")
    tokens, width = hidden.shape
    inner = w_query.shape[1]
    slots = 3 * tokens // 4
    feature_slice = w_out.shape[1] // groups
    chunks = min(CHUNKS, peers)
    rows = slots // chunks
    ring = groups // 2
    per_chunk = peers // chunks
    bn = 256 if inner % 256 == 0 else HD
    halves = 2 if feature_slice % (2 * HD) == 0 else 1
    half = feature_slice // halves
    rope = np.stack(rope_tables(tokens))
    dma = pltpu.SemaphoreType.DMA
    bf16 = jnp.bfloat16
    vmem = pl.BlockSpec(memory_space=VMEM)
    far = pl.BlockSpec(memory_space=ANY)
    line = lambda v: v.reshape(1, tokens)
    placed = pl.pallas_call(
        functools.partial(layer_kernel, peers, groups, per_chunk, bn),
        out_shape=jax.ShapeDtypeStruct((slots, feature_slice), bf16),
        in_specs=[vmem] * 4 + [far] * 6,
        out_specs=far,
        scratch_shapes=[
            VMEM((tokens, width), bf16),
            VMEM((3, width, bn), bf16),
            VMEM((3, tokens, inner), bf16),
            VMEM((groups, halves, inner, half), bf16),
            VMEM((halves, tokens, half), bf16),
            VMEM((2, tokens, HD), jnp.float32),
            VMEM((1, tokens), jnp.int32),
            VMEM((rows, tokens), bf16),
            VMEM((rows, tokens), jnp.float32),
            VMEM((rows, inner), bf16),
            VMEM((chunks, ring, halves, rows, half), bf16),
            VMEM((chunks, ring, halves, rows, half), bf16),
            VMEM((chunks, ring - 1, halves, rows, half), bf16),
            VMEM((chunks, ring - 1, halves, rows, half), bf16),
            VMEM((LAG + 1, halves, rows, half), jnp.float32),
            VMEM((chunks, halves, rows, half), bf16),
            dma((tokens // LOAD_ROWS,)),
            dma((3,)),
            dma((groups, halves)),
            dma((halves,)),
            dma,
            dma((chunks, ring, halves)),
            dma((chunks, ring, halves)),
            dma((chunks, ring - 1, halves)),
            dma((chunks, ring - 1, halves)),
            dma((chunks, per_chunk, halves)),
            dma((chunks, per_chunk, halves)),
            dma((halves,)),
        ],
        compiler_params=pltpu.CompilerParams(
            collective_id=0, has_side_effects=True, vmem_limit_bytes=60 * 2**20
        ),
        name="layer",
    )(
        line(exit_depth), line(seq_ids), line(dest), norm_gain, rope,
        hidden, w_query, w_key, w_value, w_out,
    )
    pieces = 4
    return pl.pallas_call(
        place_kernel,
        out_shape=jax.ShapeDtypeStruct((slots, feature_slice), bf16),
        in_specs=[far],
        out_specs=far,
        scratch_shapes=[
            VMEM((pieces, slots // pieces, feature_slice), bf16),
            dma((pieces,)),
            dma((pieces,)),
        ],
        name="place",
    )(placed)


def solution(mesh):
    return jax.shard_map(
        body,
        mesh=mesh,
        in_specs=(
            P("dp", None),
            P("dp"),
            P("dp"),
            P("dp"),
            P(),
            P(None, "mp"),
            P(None, "mp"),
            P(None, "mp"),
            P("mp", None),
        ),
        out_specs=P("dp", "mp"),
        check_vma=False,
    )
```
